32 devices in a mesh: grp: 4 (over x, core), gx: 4 (over z), gy: 2 (over y).
Axes of the slice: x: 2, y: 2, z: 4, core: 2. Of those that a mesh axis runs over, the one named last changes fastest.
Arguments:
- solid_velocity: float32 [3, 16, 64, 1024], P(None, 'grp', 'gx', 'gy'), may hold values from -6 to 6
- solid_stress: float32 [6, 16, 64, 1024], P(None, 'grp', 'gx', 'gy'), may hold values from -6 to 6
- ocean_pressure: float32 [8, 64, 1024], P(None, 'gx', ('grp', 'gy')), may hold values from -6 to 6
- ocean_velocity: float32 [3, 8, 64, 1024], P(None, None, 'gx', ('grp', 'gy')), may hold values from -4 to 4
- surface: float32 [64, 1024], P('gx', ('grp', 'gy')), may hold values from -6 to 6
- materials: float32 [3, 8], replicated, may hold values from 0.5 to 1.5
- region_ids: int32 [16, 64, 1024], P('grp', 'gx', 'gy'), may hold values from 0 to 7
- fault_mask: int32 [16, 64, 1024], P('grp', 'gx', 'gy'), may hold values 0 or 1
- plastic_params: float32 [2], replicated, may hold values from 0.3 to 0.6
Outputs:
- velocity_out: float32 [3, 16, 64, 1024], P(None, 'grp', 'gx', 'gy')
- stress_out: float32 [6, 16, 64, 1024], P(None, 'grp', 'gx', 'gy')
- pressure_out: float32 [8, 64, 1024], P(None, 'gx', ('grp', 'gy'))
- flow_out: float32 [3, 8, 64, 1024], P(None, None, 'gx', ('grp', 'gy'))
- surface_out: float32 [64, 1024], P('gx', ('grp', 'gy'))
The draws below stay inside these ranges and needn't reach their ends.
All inputs are finite; a program needn't handle non-finite values. No bound on the sum of `fault_mask` on one device may be relied on, other than what follows from the above.
Results may differ from the reference program's by a relative error of at most 0.00002.
Values sent between devices are 32-bit elements; how exact they have to be, the bound alone decides.
No kernel may reach another device: no remote copies, remote signals or barrier semaphores. Data moves between devices by JAX's collectives and lax.ppermute only.
A program may use at most 64 MiB of HBM per device.

```python
import jax
import jax.numpy as jnp
from jax import lax

OZ = 8
STEPS = 2
REGIONS = 8
NZ = 16
NX = 64
NY = 1024


def place_ends(array, key, smallest, largest):
    longest = array.shape.index(max(array.shape))
    spots = []
    for shift in (0, 1):
        where = [jax.random.randint(jax.random.fold_in(key, axis), (), 0, length) for axis, length in enumerate(array.shape)]
        where[longest] = (where[longest] + shift) % array.shape[longest]
        spots.append(tuple(where))
    return array.at[spots[0]].set(smallest).at[spots[1]].set(largest)


def level_of(key, dims, split, smallest, high):
    def one(axis_at, blocks):
        draws = jax.random.uniform(jax.random.fold_in(jax.random.fold_in(key, 6), axis_at), (blocks,), jnp.float32, smallest / len(split), high / len(split))
        return jnp.repeat(jnp.exp(draws), dims[axis_at] // blocks).reshape((-1,) + (1,) * (len(dims) - axis_at - 1))

    loudness = one(*split[0])
    for cut in split[1:]:
        loudness = loudness * one(*cut)
    return loudness


def centred(key, dims, width, limit, shards=(), dtype=jnp.bfloat16):
    gain = level_of(key, dims, shards, -0.22, 0.18) if shards else 1.0
    array = jax.random.normal(key, dims, jnp.float32) * width * gain
    return jnp.minimum(jnp.maximum(array, -limit), limit).astype(dtype)


def setup_inputs(seed: int = 0) -> dict:
    seeds = jax.random.split(jax.random.key(seed), 10)
    return {
        "solid_velocity": centred(seeds[0], (3, NZ, NX, NY), 1.0, 6.0, ((1, 4), (2, 4), (3, 2)), jnp.float32),
        "solid_stress": centred(seeds[1], (6, NZ, NX, NY), 1.0, 6.0, ((1, 4), (2, 4), (3, 2)), jnp.float32),
        "ocean_pressure": centred(seeds[2], (OZ, NX, NY), 1.0, 6.0, ((1, 4), (2, 8)), jnp.float32),
        "ocean_velocity": centred(seeds[3], (3, OZ, NX, NY), 0.5, 4.0, ((2, 4), (3, 8)), jnp.float32),
        "surface": centred(seeds[4], (NX, NY), 1.0, 6.0, ((0, 4), (1, 8)), jnp.float32),
        "materials": jnp.clip(jax.random.uniform(seeds[5], (3, REGIONS), jnp.float32, 0.5, 1.5), 0.5, 1.5),
        "region_ids": place_ends(jax.random.randint(seeds[6], (NZ, NX, NY), 0, REGIONS), jax.random.fold_in(seeds[6], 1), 0, REGIONS - 1).astype(jnp.int32),
        "fault_mask": place_ends((jax.random.randint(seeds[7], (NZ, NX, NY), 0, 3) < 1).astype(jnp.int32), jax.random.fold_in(seeds[7], 1), 0, 1),
        "plastic_params": jnp.clip(jax.random.uniform(seeds[8], (2,), jnp.float32, 0.3, 0.6), 0.3, 0.6),
    }


courant_number = 0.2
ocean_step = 0.3
vertical_step = 0.3
gravity_term = 0.5
surface_step = 0.3

def before(field, axis):
    widths = [(0, 0)] * field.ndim
    widths[axis] = (1, 0)
    return lax.slice_in_dim(jnp.pad(field, widths), 0, field.shape[axis], axis=axis)

def after(field, axis):
    widths = [(0, 0)] * field.ndim
    widths[axis] = (0, 1)
    return lax.slice_in_dim(jnp.pad(field, widths), 1, field.shape[axis] + 1, axis=axis)

def lookup(region_ids, row_values):
    total = jnp.zeros(region_ids.shape, jnp.float32)
    for region in range(REGIONS):
        total = total + jnp.where(region_ids == region, row_values[region], jnp.zeros((), jnp.float32))
    return total

def yield_cap(stress_xx_part, stress_yy_part, stress_zz_part, sxy, sxz, syz, fault_mask, plastic_params):
    mean = (stress_xx_part + stress_yy_part + stress_zz_part) / 3.0
    dxx, dyy, dzz = (stress_xx_part - mean, stress_yy_part - mean, stress_zz_part - mean)
    tau = jnp.sqrt(0.5 * (dxx * dxx + dyy * dyy + dzz * dzz) + sxy * sxy + sxz * sxz + syz * syz)
    strength = plastic_params[0] + plastic_params[1] * jnp.maximum(-mean, 0.0)
    factor = strength / jnp.maximum(tau, strength)
    factor = jnp.where(fault_mask == 1, factor, jnp.ones((), jnp.float32))
    return (mean + dxx * factor, mean + dyy * factor, mean + dzz * factor, sxy * factor, sxz * factor, syz * factor)

def reference(solid_velocity, solid_stress, ocean_pressure, ocean_velocity, surface, materials, region_ids, fault_mask, plastic_params):
    lame_lambda = lookup(region_ids, materials[0])
    shear_modulus = lookup(region_ids, materials[1])
    buoy = lookup(region_ids, materials[2])
    vx, vy, vz = (solid_velocity[0], solid_velocity[1], solid_velocity[2])
    stress_xx_part, stress_yy_part, stress_zz_part, sxy, sxz, syz = [solid_stress[k] for k in range(6)]
    press = ocean_pressure
    flow_x, flow_y, lift = (ocean_velocity[0], ocean_velocity[1], ocean_velocity[2])
    height = surface
    for step in range(STEPS):
        szz_above = jnp.concatenate([-press[0][None], stress_zz_part[:-1]], axis=0)
        div_x = stress_xx_part - before(stress_xx_part, 1) + (sxy - before(sxy, 2)) + (sxz - before(sxz, 0))
        div_y = sxy - before(sxy, 1) + (stress_yy_part - before(stress_yy_part, 2)) + (syz - before(syz, 0))
        div_z = sxz - before(sxz, 1) + (syz - before(syz, 2)) + (stress_zz_part - szz_above)
        vx = vx + courant_number * buoy * div_x
        vy = vy + courant_number * buoy * div_y
        vz = vz + courant_number * buoy * div_z
        gradient_xx_part, gxy, gxz = (after(vx, 1) - vx, after(vx, 2) - vx, after(vx, 0) - vx)
        gyx, gradient_yy_part, gyz = (after(vy, 1) - vy, after(vy, 2) - vy, after(vy, 0) - vy)
        gzx, gzy, gradient_zz_part = (after(vz, 1) - vz, after(vz, 2) - vz, after(vz, 0) - vz)
        dilatation = gradient_xx_part + gradient_yy_part + gradient_zz_part
        stress_xx_part = stress_xx_part + courant_number * (lame_lambda * dilatation + 2.0 * shear_modulus * gradient_xx_part)
        stress_yy_part = stress_yy_part + courant_number * (lame_lambda * dilatation + 2.0 * shear_modulus * gradient_yy_part)
        stress_zz_part = stress_zz_part + courant_number * (lame_lambda * dilatation + 2.0 * shear_modulus * gradient_zz_part)
        sxy = sxy + courant_number * shear_modulus * (gxy + gyx)
        sxz = sxz + courant_number * shear_modulus * (gxz + gzx)
        syz = syz + courant_number * shear_modulus * (gyz + gzy)
        stress_xx_part, stress_yy_part, stress_zz_part, sxy, sxz, syz = yield_cap(stress_xx_part, stress_yy_part, stress_zz_part, sxy, sxz, syz, fault_mask, plastic_params)
        flow_x = flow_x - ocean_step * (after(press, 1) - press)
        flow_y = flow_y - ocean_step * (after(press, 2) - press)
        above = jnp.concatenate([press[1:], (gravity_term * height)[None]], axis=0)
        lift = lift - vertical_step * (above - press)
        lift_below = jnp.concatenate([vz[0][None], lift[:-1]], axis=0)
        press = press - ocean_step * (flow_x - before(flow_x, 1) + (flow_y - before(flow_y, 2))) - vertical_step * (lift - lift_below)
        height = height + surface_step * lift[-1]
    return (jnp.stack([vx, vy, vz]), jnp.stack([stress_xx_part, stress_yy_part, stress_zz_part, sxy, sxz, syz]), press, jnp.stack([flow_x, flow_y, lift]), height)
```

```python
import jax
import jax.numpy as jnp
from jax import lax
from jax.experimental import pallas as pl
from jax.experimental.pallas import tpu as pltpu
from jax.sharding import PartitionSpec as P

STEPS = 2
REGIONS = 8


courant_number = 0.2
ocean_step = 0.3
vertical_step = 0.3
gravity_term = 0.5
surface_step = 0.3


def from_behind(value, axis, steps):
    count = lax.axis_size(axis)
    first, last = (max(0, -steps), min(count, count - steps))
    return lax.ppermute(value, axis, [(source, source + steps) for source in range(first, last)])


def lookup(region_ids, row_values):
    total = jnp.zeros(region_ids.shape, jnp.float32)
    for region in range(REGIONS):
        total = total + jnp.where(
            region_ids == region, row_values[region], jnp.zeros((), jnp.float32)
        )
    return total


def yield_cap(
    stress_xx_part, stress_yy_part, stress_zz_part, sxy, sxz, syz, fault_mask, plastic_params
):
    mean = (stress_xx_part + stress_yy_part + stress_zz_part) / 3.0
    dxx, dyy, dzz = (stress_xx_part - mean, stress_yy_part - mean, stress_zz_part - mean)
    tau = jnp.sqrt(0.5 * (dxx * dxx + dyy * dyy + dzz * dzz) + sxy * sxy + sxz * sxz + syz * syz)
    strength = plastic_params[0] + plastic_params[1] * jnp.maximum(-mean, 0.0)
    factor = strength / jnp.maximum(tau, strength)
    factor = jnp.where(fault_mask == 1, factor, jnp.ones((), jnp.float32))
    return (
        mean + dxx * factor,
        mean + dyy * factor,
        mean + dzz * factor,
        sxy * factor,
        sxz * factor,
        syz * factor,
    )


def with_before(field, face, axis):
    rest = lax.slice_in_dim(field, 0, field.shape[axis] - 1, axis=axis)
    return jnp.concatenate([face, rest], axis=axis)


def with_after(field, face, axis):
    rest = lax.slice_in_dim(field, 1, field.shape[axis], axis=axis)
    return jnp.concatenate([rest, face], axis=axis)


def pick_slots(quarters, wanted):
    slots = jnp.zeros((wanted.shape[0], quarters.shape[0], quarters.shape[2]), jnp.float32)
    for quarter in range(quarters.shape[1]):
        keep = wanted[:, quarter][:, None, None]
        slots = slots + jnp.where(keep, quarters[None, :, quarter, :], jnp.zeros((), jnp.float32))
    return slots


def assemble(received, owned, ranks, n_grp):
    pieces = []
    for quarter in range(n_grp):
        keep = (owned & (ranks % n_grp == quarter))[:, None, None]
        pieces.append(jnp.sum(jnp.where(keep, received, jnp.zeros((), jnp.float32)), axis=0))
    whole = jnp.stack(pieces, axis=1)
    return whole.reshape(whole.shape[0], whole.shape[1] * whole.shape[2])


def seafloor_to_ocean(slab):
    n_grp = lax.axis_size("grp")
    n_gy = lax.axis_size("gy")
    group = lax.axis_index("grp")
    column = lax.axis_index("gy")
    width = slab.shape[1] // n_grp
    quarter_ids = jnp.arange(n_grp)
    quarters = slab.reshape(slab.shape[0], n_grp, width)
    ranks = jnp.arange(n_grp * n_gy)
    owned = (ranks // n_grp == column) & (group == 0)
    wanted = owned[:, None] & ((ranks % n_grp)[:, None] == quarter_ids[None, :])
    received = lax.all_to_all(
        pick_slots(quarters, wanted), ("grp", "gy"), split_axis=0, concat_axis=0, tiled=True
    )
    return jnp.sum(received, axis=0)


def pressure_to_solid(bottom):
    n_grp = lax.axis_size("grp")
    n_gy = lax.axis_size("gy")
    group = lax.axis_index("grp")
    column = lax.axis_index("gy")
    rank = group * n_gy + column
    targets = jnp.arange(n_grp * n_gy) == rank // n_grp
    slots = jnp.where(targets[:, None, None], bottom[None], jnp.zeros((), jnp.float32))
    received = lax.all_to_all(slots, ("grp", "gy"), split_axis=0, concat_axis=0, tiled=True)
    ranks = jnp.arange(n_grp * n_gy)
    owned = (ranks // n_grp == column) & (group == 0)
    return assemble(received, owned, ranks, n_grp)


def body(
    solid_velocity,
    solid_stress,
    ocean_pressure,
    ocean_velocity,
    surface,
    materials,
    region_ids,
    fault_mask,
    plastic_params,
):
    is_top = (lax.axis_index("grp") == 0).astype(jnp.float32)
    lame_lambda = lookup(region_ids, materials[0])
    shear_modulus = lookup(region_ids, materials[1])
    buoy = lookup(region_ids, materials[2])
    vx, vy, vz = (solid_velocity[0], solid_velocity[1], solid_velocity[2])
    stress_xx_part, stress_yy_part, stress_zz_part, sxy, sxz, syz = [
        solid_stress[k] for k in range(6)
    ]
    press = ocean_pressure
    flow_x, flow_y, lift = (ocean_velocity[0], ocean_velocity[1], ocean_velocity[2])
    height = surface
    for step in range(STEPS):
        load = pressure_to_solid(press[0]) * is_top
        face_x = from_behind(
            jnp.stack([stress_xx_part[:, -1:, :], sxy[:, -1:, :], sxz[:, -1:, :]]), "gx", 1
        )
        face_y = from_behind(
            jnp.stack([sxy[:, :, -1:], stress_yy_part[:, :, -1:], syz[:, :, -1:]]), "gy", 1
        )
        face_z = from_behind(jnp.stack([sxz[-1:], syz[-1:], stress_zz_part[-1:]]), "grp", 1)
        szz_face = face_z[2] - load[None]
        div_x = (
            stress_xx_part
            - with_before(stress_xx_part, face_x[0], 1)
            + (sxy - with_before(sxy, face_y[0], 2))
            + (sxz - with_before(sxz, face_z[0], 0))
        )
        div_y = (
            sxy
            - with_before(sxy, face_x[1], 1)
            + (stress_yy_part - with_before(stress_yy_part, face_y[1], 2))
            + (syz - with_before(syz, face_z[1], 0))
        )
        div_z = (
            sxz
            - with_before(sxz, face_x[2], 1)
            + (syz - with_before(syz, face_y[2], 2))
            + (stress_zz_part - with_before(stress_zz_part, szz_face, 0))
        )
        vx = vx + courant_number * buoy * div_x
        vy = vy + courant_number * buoy * div_y
        vz = vz + courant_number * buoy * div_z
        motion = jnp.stack([vx, vy, vz])
        next_x = from_behind(motion[:, :, :1, :], "gx", -1)
        next_y = from_behind(motion[:, :, :, :1], "gy", -1)
        next_z = from_behind(motion[:, :1], "grp", -1)
        gradient_xx_part, gxy, gxz = (
            with_after(vx, next_x[0], 1) - vx,
            with_after(vx, next_y[0], 2) - vx,
            with_after(vx, next_z[0], 0) - vx,
        )
        gyx, gradient_yy_part, gyz = (
            with_after(vy, next_x[1], 1) - vy,
            with_after(vy, next_y[1], 2) - vy,
            with_after(vy, next_z[1], 0) - vy,
        )
        gzx, gzy, gradient_zz_part = (
            with_after(vz, next_x[2], 1) - vz,
            with_after(vz, next_y[2], 2) - vz,
            with_after(vz, next_z[2], 0) - vz,
        )
        dilatation = gradient_xx_part + gradient_yy_part + gradient_zz_part
        stress_xx_part = stress_xx_part + courant_number * (
            lame_lambda * dilatation + 2.0 * shear_modulus * gradient_xx_part
        )
        stress_yy_part = stress_yy_part + courant_number * (
            lame_lambda * dilatation + 2.0 * shear_modulus * gradient_yy_part
        )
        stress_zz_part = stress_zz_part + courant_number * (
            lame_lambda * dilatation + 2.0 * shear_modulus * gradient_zz_part
        )
        sxy = sxy + courant_number * shear_modulus * (gxy + gyx)
        sxz = sxz + courant_number * shear_modulus * (gxz + gzx)
        syz = syz + courant_number * shear_modulus * (gyz + gzy)
        stress_xx_part, stress_yy_part, stress_zz_part, sxy, sxz, syz = yield_cap(
            stress_xx_part,
            stress_yy_part,
            stress_zz_part,
            sxy,
            sxz,
            syz,
            fault_mask,
            plastic_params,
        )
        floor_lift = seafloor_to_ocean(vz[0])
        press_x = from_behind(press[:, :1, :], "gx", -1)
        press_y = from_behind(press[:, :, :1], ("grp", "gy"), -1)
        flow_x = flow_x - ocean_step * (with_after(press, press_x, 1) - press)
        flow_y = flow_y - ocean_step * (with_after(press, press_y, 2) - press)
        above = jnp.concatenate([press[1:], (gravity_term * height)[None]], axis=0)
        lift = lift - vertical_step * (above - press)
        lift_below = jnp.concatenate([floor_lift[None], lift[:-1]], axis=0)
        flow_prev_x = from_behind(flow_x[:, -1:, :], "gx", 1)
        flow_prev_y = from_behind(flow_y[:, :, -1:], ("grp", "gy"), 1)
        spread = (
            flow_x
            - with_before(flow_x, flow_prev_x, 1)
            + (flow_y - with_before(flow_y, flow_prev_y, 2))
        )
        press = press - ocean_step * spread - vertical_step * (lift - lift_below)
        height = height + surface_step * lift[-1]
    return (
        jnp.stack([vx, vy, vz]),
        jnp.stack([stress_xx_part, stress_yy_part, stress_zz_part, sxy, sxz, syz]),
        press,
        jnp.stack([flow_x, flow_y, lift]),
        height,
    )


FIELDS = 11
REGION, FAULT = 9, 10


def row_of(shape):
    return lax.broadcasted_iota(jnp.int32, shape, len(shape) - 2)


def lane_of(shape):
    return lax.broadcasted_iota(jnp.int32, shape, len(shape) - 1)


def turn(tile, shift, axis):
    shift %= tile.shape[axis]
    return tile if shift == 0 else pltpu.roll(tile, shift, axis)


def cell(refs, field, layer, rows):
    v_ref, s_ref, region_ref, fault_ref = refs
    if field < 3:
        return v_ref[field, layer, rows, :]
    if field < REGION:
        return s_ref[field - 3, layer, rows, :]
    if field == REGION:
        return region_ref[layer, rows, :].astype(jnp.float32) + 1.0
    return fault_ref[layer, rows, :].astype(jnp.float32)


def sea(refs, plane, rows):
    p_ref, u_ref, h_ref = refs
    layers = p_ref.shape[0]
    if plane < layers:
        return p_ref[plane, rows, :]
    if plane < 4 * layers:
        return u_ref[plane // layers - 1, plane % layers, rows, :]
    return h_ref[rows, :]


def rows_kernel(v, s, region, fault, p, u, h, first, last, up, down):
    solid, ocean = (v, s, region, fault), (p, u, h)
    layers, n, width = s.shape[1:]
    head, tail = slice(0, 8), slice(n - 8, n)
    row = row_of((8, width))
    for f in range(FIELDS):
        a = b = jnp.zeros((8, width), jnp.float32)
        for z in range(layers):
            mine = row // 2 == z
            a = jnp.where(mine, turn(cell(solid, f, z, head), 2 * z, 0), a)
            b = jnp.where(mine, turn(cell(solid, f, z, tail), 2 * z + 2, 0), b)
        first[f] = a
        last[f] = b
    w = p.shape[2]
    row = row_of((8, w))
    planes = 4 * p.shape[0] + 1
    per = width // w
    for t in range((first.shape[0] - FIELDS) * per):
        a = b = jnp.zeros((8, w), jnp.float32)
        for q in range(4):
            if 4 * t + q < planes:
                mine = row // 2 == q
                a = jnp.where(mine, turn(sea(ocean, 4 * t + q, head), 2 * q, 0), a)
                b = jnp.where(mine, turn(sea(ocean, 4 * t + q, tail), 2 * q + 2, 0), b)
        lanes = slice(t % per * w, (t % per + 1) * w)
        first[FIELDS + t // per, :, lanes] = a
        last[FIELDS + t // per, :, lanes] = b
    full = slice(0, n)
    for f in range(FIELDS):
        up[2 * f] = cell(solid, f, 0, full)
        if f < FAULT:
            up[2 * f + 1] = cell(solid, f, 1, full)
        down[3 + f] = cell(solid, f, layers - 1, full)
    for i, f in enumerate((5, 7, 8)):
        down[i] = cell(solid, f, layers - 2, full)


def columns_kernel(va, sa, ra, fa, vb, sb, rb, fb, p, u, h, solid_out, first_out, last_out):
    here = lax.axis_index("gy") == 0
    layers, n = sa.shape[1:3]
    full = slice(0, n)
    lane = lane_of((n, 128))
    total = jnp.zeros((n, 128), jnp.float32)
    for f in range(FIELDS):
        for z in range(layers):
            j = f * layers + z
            tile = jnp.where(
                here,
                turn(cell((vb, sb, rb, fb), f, z, full), 2, 1),
                cell((va, sa, ra, fa), f, z, full),
            )
            total = jnp.where(lane // 2 == j, turn(tile, 2 * j, 1), total)
    solid_out[...] = total
    a = b = jnp.zeros((n, 128), jnp.float32)
    for j in range(4 * p.shape[0] + 1):
        tile = sea((p, u, h), j, full)
        a = jnp.where(lane // 2 == j, turn(tile, 2 * j, 1), a)
        b = jnp.where(lane // 2 == j, turn(tile, 2 * j + 2, 1), b)
    first_out[...] = a
    last_out[...] = b


def rim(after, before, slot):
    row = row_of(after.shape)
    tile = jnp.where(row < 2, turn(after, -2 * slot, 0), 0.0)
    return jnp.where(row >= 6, turn(before, 6 - 2 * slot, 0), tile)


def sea_rim(after, before, plane, per):
    t, q = plane // 4, plane % 4
    lanes = slice(t % per * 128, (t % per + 1) * 128)
    k = FIELDS + t // per
    return rim(after[k, :, lanes], before[k, :, lanes], q)


def before_x(tile):
    return turn(tile, 1, 0)


def after_x(tile):
    return turn(tile, -1, 0)


def sides_kernel(after, before, solid, first, last, p, u, out):
    here = lax.axis_index("gy") == 0
    n = solid.shape[0]
    layers = after.shape[1] // 2
    width = after.shape[2]
    per = width // 128
    lane = lane_of((8, 128))
    total = jnp.zeros((8, 128), jnp.float32)
    for f in range(FIELDS):
        a = jnp.where(here, turn(after[f, :, width - 128 :], 2, 1), after[f, :, :128])
        b = jnp.where(here, turn(before[f, :, width - 128 :], 2, 1), before[f, :, :128])
        for z in range(layers):
            j = f * layers + z
            total = jnp.where(lane // 2 == j, turn(rim(a, b, z), 2 * j, 1), total)
    out[0, :n] = solid[...]
    out[0, n:] = total
    sea_layers = p.shape[0]
    a = b = jnp.zeros((8, 128), jnp.float32)
    for j in range(4 * sea_layers + 1):
        tile = sea_rim(after, before, j, per)
        a = jnp.where(lane // 2 == j, turn(tile, 2 * j, 1), a)
        b = jnp.where(lane // 2 == j, turn(tile, 2 * j + 2, 1), b)
    out[1, :n] = first[...]
    out[1, n:] = a
    out[2, :n] = last[...]
    out[2, n:] = b

    def grown(tile, plane):
        return jnp.concatenate([tile, sea_rim(after, before, plane, per)], axis=0)

    row = row_of((n + 8, 128))
    p0, p1 = grown(p[0], 0), grown(p[1], 1)
    ux = grown(u[0, 0], sea_layers) - ocean_step * (after_x(p0) - p0)
    ux = jnp.where((row == n + 7) & (lax.axis_index("gx") == 0), 0.0, ux)
    w = grown(u[2, 0], 3 * sea_layers) - vertical_step * (p1 - p0)
    out[3] = p0
    out[4] = grown(u[1, 0], 2 * sea_layers)
    out[5] = p0 - ocean_step * (ux - before_x(ux)) - vertical_step * w


def frames_kernel(after, before, mine, other, up, down, deep):
    row = row_of((8, 128))
    for f in range(FIELDS):
        for c in range(after.shape[2] // 128):
            a = after[f, :, c * 128 : (c + 1) * 128]
            b = before[f, :, c * 128 : (c + 1) * 128]
            up[4 * f + c] = jnp.where(row < 4, a, turn(b, 4, 0))
            down[4 * f + c] = jnp.where(row < 4, turn(a, 4, 0), b)
    base = 4 * FIELDS
    for i in range(3):
        rows = slice(8 * i, 8 * i + 8)
        up[base + i] = other[0, rows]
        down[base + i] = other[0, rows]
        up[base + 3 + i] = other[1, rows]
        down[base + 3 + i] = other[2, rows]
        for k in range(3):
            for m, source in enumerate((mine, other)):
                tile = source[3 + k, rows]
                place = 9 * m + 3 * k + i
                up[base + 6 + place] = tile
                down[base + 6 + place] = tile
                deep[place] = tile


def three(ref, at):
    return jnp.concatenate([ref[at], ref[at + 1], ref[at + 2]], axis=0)


def solid_kernel(
    materials, plastic, v, s, region, fault, low, high, after, before, side, mine,
    frame_low, frame_high, deep, v_out, s_out, lift_out, cells, stuff, sea_state,
):
    f32 = jnp.float32
    top = lax.axis_index("grp") == 0
    here = lax.axis_index("gy") == 0
    layers, n, width = s.shape[1:]
    chunks = width // 128
    wide = width + 128
    tall = n + 8
    solid = (v, s, region, fault)
    full = slice(0, n)
    core = slice(0, width)
    row8 = row_of((8, 128))
    lane_tall = lane_of((tall, 128))

    def side_tile(packed, j):
        tile = turn(packed, -2 * j, 1)
        a = jnp.where(here & (lane_tall < 2), tile, 0.0)
        return jnp.where(jnp.logical_not(here) & (lane_tall >= 126), turn(tile, -2, 1), a)

    side0 = side[0]
    side_low = jnp.where(top, 0.0, three(frame_low, 4 * FIELDS))
    side_high = three(frame_high, 4 * FIELDS)
    for f in range(FIELDS):
        for z in range(layers):
            cells[f, z + 2, 0:n, core] = cell(solid, f, z, full)
            cells[f, z + 2, 0:tall, width:wide] = side_tile(side0, f * layers + z)
            for c in range(chunks):
                lanes = slice(c * 128, c * 128 + 128)
                cells[f, z + 2, n:tall, lanes] = rim(after[f, :, lanes], before[f, :, lanes], z)
        for slot in (0, 1, layers + 2, layers + 3):
            if slot == 0 and f not in (5, 7, 8):
                continue
            if slot == layers + 3 and f == FAULT:
                continue
            if slot < 2:
                z = slot + layers - 2
                plane = low[(5, 7, 8).index(f)] if slot == 0 else low[3 + f]
                packed = side_low
            else:
                z = slot - layers - 2
                plane = high[2 * f + z]
                packed = side_high
            cells[f, slot, 0:n, core] = plane
            cells[f, slot, 0:tall, width:wide] = side_tile(packed, f * layers + z)
            for c in range(chunks):
                frame = (frame_low if slot < 2 else frame_high)[4 * f + c]
                place = slot % 2
                tile = jnp.where(row8 < 2, turn(frame, -2 * place, 0), 0.0)
                tile = jnp.where(row8 >= 6, turn(frame, 2 - 2 * place, 0), tile)
                if slot < 2:
                    tile = jnp.where(top, 0.0, tile)
                cells[f, slot, n:tall, c * 128 : c * 128 + 128] = tile

    def sea_tile(k, r):
        m, odd = r // 2, r % 2
        if m == 0:
            a, b = mine[3 + k], side[3 + k]
        else:
            ref = {1: frame_high, 2: deep, 3: frame_low}[m]
            base = 0 if m == 2 else 4 * FIELDS + 6
            a, b = three(ref, base + 3 * k), three(ref, base + 9 + 3 * k)
        return jnp.where(here, b, a) if odd else jnp.where(here, a, b)

    half = chunks
    for k in range(3):
        for c in range(chunks):
            sea_state[k, :, c * 128 : c * 128 + 128] = jnp.where(
                here, sea_tile(k, c), sea_tile(k, half + c)
            )
        tile = jnp.where(here & (lane_tall < 2), sea_tile(k, half), 0.0)
        sea_state[k, :, width:wide] = jnp.where(
            jnp.logical_not(here) & (lane_tall >= 126), sea_tile(k, half - 1), tile
        )
    for c in range(chunks + 1):
        lanes = slice(c * 128, c * 128 + 128)
        cells[5, 1, :, lanes] = jnp.where(top, -sea_state[0, :, lanes], cells[5, 1, :, lanes])

    def look(z, carry):
        for c in range(chunks + 1):
            lanes = slice(c * 128, c * 128 + 128)
            region_tile = cells[REGION, z, :, lanes]
            out = [jnp.zeros((tall, 128), f32)] * 3
            for r in range(REGIONS):
                hit = region_tile == float(r + 1)
                out = [jnp.where(hit, materials[k, r], out[k]) for k in range(3)]
            stuff[0, z, :, lanes] = out[0]
            stuff[1, z, :, lanes] = out[1]
            stuff[2, z, :, lanes] = courant_number * out[2]
        return carry

    lax.fori_loop(1, layers + 4, look, 0)

    def before_y(tile, neighbour):
        return jnp.where(lane_of(tile.shape) == 0, turn(neighbour, 1, 1), turn(tile, 1, 1))

    def after_y(tile, neighbour):
        return jnp.where(lane_of(tile.shape) == 127, turn(neighbour, -1, 1), turn(tile, -1, 1))

    def lanes_of(c):
        c %= chunks + 1
        return slice(c * 128, c * 128 + 128)

    def velocity(z, carry):
        for c in range(chunks + 1):
            lanes, behind = lanes_of(c), lanes_of(c - 1)
            xx, yy, zz, xy, xz, yz = [cells[3 + k, z, :, lanes] for k in range(6)]
            gain = stuff[2, z, :, lanes]
            div_x = (
                (xx - before_x(xx))
                + (xy - before_y(xy, cells[6, z, :, behind]))
                + (xz - cells[7, z - 1, :, lanes])
            )
            div_y = (
                (xy - before_x(xy))
                + (yy - before_y(yy, cells[4, z, :, behind]))
                + (yz - cells[8, z - 1, :, lanes])
            )
            div_z = (
                (xz - before_x(xz))
                + (yz - before_y(yz, cells[8, z, :, behind]))
                + (zz - cells[5, z - 1, :, lanes])
            )
            cells[0, z, :, lanes] = cells[0, z, :, lanes] + gain * div_x
            cells[1, z, :, lanes] = cells[1, z, :, lanes] + gain * div_y
            cells[2, z, :, lanes] = cells[2, z, :, lanes] + gain * div_z
        return carry

    cohesion, friction = plastic[0], plastic[1]

    def stress(z, c, rows):
        lanes, ahead = lanes_of(c), lanes_of(c + 1)
        vx, vy, vz = [cells[k, z, :, lanes] for k in range(3)]
        nx, ny, nz = [cells[k, z, :, ahead] for k in range(3)]
        bx, by, bz = [cells[k, z + 1, :, lanes] for k in range(3)]
        keep = slice(0, rows)

        def cut(tile):
            return tile[keep]

        gxx, gxy, gxz = cut(after_x(vx) - vx), cut(after_y(vx, nx) - vx), cut(bx - vx)
        gyx, gyy, gyz = cut(after_x(vy) - vy), cut(after_y(vy, ny) - vy), cut(by - vy)
        gzx, gzy, gzz = cut(after_x(vz) - vz), cut(after_y(vz, nz) - vz), cut(bz - vz)
        lam = stuff[0, z, keep, lanes]
        mu = stuff[1, z, keep, lanes]
        xx, yy, zz, xy, xz, yz = [cells[3 + k, z, keep, lanes] for k in range(6)]
        swell = lam * (gxx + gyy + gzz)
        two = 2.0 * mu
        xx = xx + courant_number * (swell + two * gxx)
        yy = yy + courant_number * (swell + two * gyy)
        zz = zz + courant_number * (swell + two * gzz)
        shear = courant_number * mu
        xy = xy + shear * (gxy + gyx)
        xz = xz + shear * (gxz + gzx)
        yz = yz + shear * (gyz + gzy)
        mean = (xx + yy + zz) / 3.0
        dxx, dyy, dzz = xx - mean, yy - mean, zz - mean
        tau = jnp.sqrt(
            0.5 * (dxx * dxx + dyy * dyy + dzz * dzz) + xy * xy + xz * xz + yz * yz
        )
        strength = cohesion + friction * jnp.maximum(-mean, 0.0)
        factor = strength / jnp.maximum(tau, strength)
        factor = jnp.where(cells[FAULT, z, keep, lanes] == 1.0, factor, 1.0)
        return (
            mean + dxx * factor,
            mean + dyy * factor,
            mean + dzz * factor,
            xy * factor,
            xz * factor,
            yz * factor,
        )

    def first_stress(z, carry):
        for c in range(chunks + 1):
            for k, tile in enumerate(stress(z, c, tall)):
                cells[3 + k, z, :, lanes_of(c)] = tile
        return carry

    def last_stress(z, carry):
        for c in range(chunks):
            for k, tile in enumerate(stress(z, c, n)):
                s_out[k, z - 2, :, lanes_of(c)] = tile
        return carry

    lax.fori_loop(1, layers + 4, velocity, 0)
    for c in range(chunks + 1):
        sea_state[3, :, lanes_of(c)] = cells[2, 2, :, lanes_of(c)]
        p0 = sea_state[0, :, lanes_of(c)]
        uy = sea_state[1, :, lanes_of(c)] - ocean_step * (
            after_y(p0, sea_state[0, :, lanes_of(c + 1)]) - p0
        )
        sea_state[1, :, lanes_of(c)] = jnp.where(cells[REGION, 2, :, lanes_of(c)] > 0.5, uy, 0.0)
    lax.fori_loop(1, layers + 3, first_stress, 0)
    for c in range(chunks + 1):
        uy = sea_state[1, :, lanes_of(c)]
        press = (
            sea_state[2, :, lanes_of(c)]
            - ocean_step * (uy - before_y(uy, sea_state[1, :, lanes_of(c - 1)]))
            + vertical_step * sea_state[3, :, lanes_of(c)]
        )
        cells[5, 1, :, lanes_of(c)] = jnp.where(top, -press, cells[5, 1, :, lanes_of(c)])
    lax.fori_loop(2, layers + 3, velocity, 0)
    for k in range(3):
        for z in range(layers):
            v_out[k, z] = cells[k, z + 2, 0:n, core]
    lax.fori_loop(2, layers + 2, last_stress, 0)
    for c in range(chunks):
        ahead, behind = sea_state[3, :, lanes_of(c + 1)], sea_state[3, :, lanes_of(c - 1)]
        lift_out[c, 0] = sea_state[3, :, lanes_of(c)]
        lift_out[c, 1] = jnp.where(lane_tall == 0, ahead, jnp.where(lane_tall == 127, behind, 0.0))
        lift_out[c, 2] = cells[2, 2, :, lanes_of(c)]


def ocean_kernel(
    p, u, h, after, before, side, frame_low, frame_high, la, lb, lc, ld,
    p_out, u_out, h_out, ext,
):
    here = lax.axis_index("gy") == 0
    group, groups = lax.axis_index("grp"), lax.axis_size("grp")
    column, columns = lax.axis_index("gy"), lax.axis_size("gy")
    strike, strikes = lax.axis_index("gx"), lax.axis_size("gx")
    rank = group * columns + column
    layers, n, w = p.shape
    tall, wide = n + 8, 2 * w
    per = after.shape[2] // 128
    row, lane = row_of((tall, wide)), lane_of((tall, wide))
    small = lane_of((tall, w))
    inside = jnp.logical_not((row == n) & (strike == strikes - 1))
    inside &= jnp.logical_not((row == tall - 1) & (strike == 0))
    inside &= jnp.logical_not((lane == w) & (rank == groups * columns - 1))
    inside &= jnp.logical_not((lane == wide - 1) & (rank == 0))
    at = 4 * FIELDS + 3
    ahead = jnp.where(here, side[1], three(frame_high, at))
    behind = jnp.where(here, jnp.where(group == 0, 0.0, three(frame_low, at)), side[2])

    def grown(plane):
        tile = jnp.concatenate(
            [sea((p, u, h), plane, slice(0, n)), sea_rim(after, before, plane, per)], axis=0
        )
        edge = jnp.where(small < 2, turn(ahead, -2 * plane, 1), 0.0)
        edge = jnp.where(small >= 126, turn(behind, 126 - 2 * plane, 1), edge)
        return jnp.concatenate([tile, edge], axis=1)

    for j in range(4 * layers + 1):
        ext[j] = grown(j)

    def shifted(tile, shift, axis):
        return turn(tile, shift, axis)

    def moved(press, flow, axis):
        flow = flow - ocean_step * (shifted(press, -1, axis) - press)
        return jnp.where(inside, flow, 0.0)

    for step in range(STEPS):
        final = step == STEPS - 1
        if step == 0:
            below = jnp.concatenate(
                [la[0] + lb[0] + lc[0] + ld[0], la[1] + lb[1] + lc[1] + ld[1]], axis=1
            )
        else:
            below = jnp.concatenate(
                [la[2] + lb[2] + lc[2] + ld[2], jnp.zeros((tall, w), jnp.float32)], axis=1
            )
        height = ext[4 * layers]
        for k in range(layers):
            press = ext[k]
            ux = moved(press, ext[layers + k], 0)
            uy = moved(press, ext[2 * layers + k], 1)
            above = gravity_term * height if k == layers - 1 else ext[k + 1]
            lift = ext[3 * layers + k] - vertical_step * (above - press)
            spread = ux - shifted(ux, 1, 0) + (uy - shifted(uy, 1, 1))
            press = press - ocean_step * spread - vertical_step * (lift - below)
            below = lift
            if final:
                p_out[k] = press[:n, :w]
                u_out[0, k] = ux[:n, :w]
                u_out[1, k] = uy[:n, :w]
                u_out[2, k] = lift[:n, :w]
            else:
                ext[k] = jnp.where(inside, press, 0.0)
                ext[layers + k] = ux
                ext[2 * layers + k] = uy
                ext[3 * layers + k] = lift
        height = height + surface_step * below
        if final:
            h_out[...] = height[:n, :w]
        else:
            ext[4 * layers] = height


def call(kernel, shapes, inputs, specs=None, scratch=(), smem=0, name=None):
    vmem = pl.BlockSpec(memory_space=pltpu.VMEM)
    if specs is None:
        specs = [pl.BlockSpec(memory_space=pltpu.SMEM)] * smem + [vmem] * (len(inputs) - smem)
    outs = [jax.ShapeDtypeStruct(shape, jnp.float32) for shape in shapes]
    return pl.pallas_call(
        kernel,
        out_shape=outs,
        in_specs=specs,
        out_specs=[vmem] * len(outs),
        scratch_shapes=list(scratch),
        compiler_params=pltpu.CompilerParams(vmem_limit_bytes=48 * 1024 * 1024),
        name=name,
    )(*inputs)


def fast_body(v, s, p, u, h, materials, region, fault, plastic):
    layers, n, width = s.shape[1:]
    sea_layers, _, w = p.shape
    tall, wide = n + 8, width + 128
    planes = 4 * sea_layers + 1
    slabs = FIELDS + -(-planes // (4 * (width // w)))
    n_grp, n_gy = lax.axis_size("grp"), lax.axis_size("gy")
    first, last, up, down = call(
        rows_kernel,
        [(slabs, 8, width), (slabs, 8, width), (2 * FIELDS - 1, n, width), (FIELDS + 3, n, width)],
        (v, s, region, fault, p, u, h),
        name="rows",
    )
    after = from_behind(first, "gx", -1)
    before = from_behind(last, "gx", 1)
    high = from_behind(up, "grp", -1)
    low = from_behind(down, "grp", 1)
    edges = (
        [a[..., :128] for a in (v, s, region, fault)]
        + [a[..., width - 128 :] for a in (v, s, region, fault)]
    )
    own = call(columns_kernel, [(n, 128)] * 3, (*edges, p, u, h), name="columns")
    (mine,) = call(sides_kernel, [(6, tall, 128)], (after, before, *own, p, u), name="sides")
    side = lax.ppermute(mine, "gy", [(i, n_gy - 1 - i) for i in range(n_gy)])
    tiles = 4 * FIELDS + 24
    frame_up, frame_down, deep = call(
        frames_kernel,
        [(tiles, 8, 128), (tiles, 8, 128), (18, 8, 128)],
        (after, before, mine, side),
        name="frames",
    )
    deep = lax.ppermute(deep, "grp", [(2, 0)])
    frame_low = lax.ppermute(frame_down, "grp", [(i, (i + 1) % n_grp) for i in range(n_grp)])
    frame_high = from_behind(frame_up, "grp", -1)
    v_out, s_out, lift = call(
        solid_kernel,
        [v.shape, s.shape, (width // w, 3, tall, w)],
        (
            materials, plastic, v, s, region, fault, low, high, after, before, side, mine,
            frame_low, frame_high, deep,
        ),
        scratch=[
            pltpu.VMEM((FIELDS, layers + 4, tall, wide), jnp.float32),
            pltpu.VMEM((3, layers + 4, tall, wide), jnp.float32),
            pltpu.VMEM((4, tall, wide), jnp.float32),
        ],
        smem=2,
        name="solid",
    )
    lifts = [
        lax.ppermute(
            lift[k], ("grp", "gy"), [(r // n_grp, r) for r in range(k, n_grp * n_gy, n_grp)]
        )
        for k in range(n_grp)
    ]
    p_out, u_out, h_out = call(
        ocean_kernel,
        [p.shape, u.shape, h.shape],
        (p, u, h, after, before, side, frame_low, frame_high, *lifts),
        scratch=[pltpu.VMEM((planes, tall, 2 * w), jnp.float32)],
        name="ocean",
    )
    return v_out, s_out, p_out, u_out, h_out


def solution(mesh):
    placed = (
        P(None, "grp", "gx", "gy"),
        P(None, "grp", "gx", "gy"),
        P(None, "gx", ("grp", "gy")),
        P(None, None, "gx", ("grp", "gy")),
        P("gx", ("grp", "gy")),
        P(),
        P("grp", "gx", "gy"),
        P("grp", "gx", "gy"),
        P(),
    )
    relay = mesh.shape["gy"] == 2 and mesh.shape["grp"] == 4
    return jax.shard_map(
        fast_body if relay else body,
        mesh=mesh,
        in_specs=placed,
        out_specs=(
            P(None, "grp", "gx", "gy"),
            P(None, "grp", "gx", "gy"),
            P(None, "gx", ("grp", "gy")),
            P(None, None, "gx", ("grp", "gy")),
            P("gx", ("grp", "gy")),
        ),
        check_vma=False,
    )
```

```python
import jax
import jax.numpy as jnp
from jax import lax
from jax.experimental import pallas as pl
from jax.experimental.pallas import tpu as pltpu
from jax.sharding import PartitionSpec as P

STEPS = 2
REGIONS = 8


courant_number = 0.2
ocean_step = 0.3
vertical_step = 0.3
gravity_term = 0.5
surface_step = 0.3


def from_behind(value, axis, steps):
    count = lax.axis_size(axis)
    first, last = (max(0, -steps), min(count, count - steps))
    return lax.ppermute(value, axis, [(source, source + steps) for source in range(first, last)])


def lookup(region_ids, row_values):
    total = jnp.zeros(region_ids.shape, jnp.float32)
    for region in range(REGIONS):
        total = total + jnp.where(
            region_ids == region, row_values[region], jnp.zeros((), jnp.float32)
        )
    return total


def yield_cap(
    stress_xx_part, stress_yy_part, stress_zz_part, sxy, sxz, syz, fault_mask, plastic_params
):
    mean = (stress_xx_part + stress_yy_part + stress_zz_part) / 3.0
    dxx, dyy, dzz = (stress_xx_part - mean, stress_yy_part - mean, stress_zz_part - mean)
    tau = jnp.sqrt(0.5 * (dxx * dxx + dyy * dyy + dzz * dzz) + sxy * sxy + sxz * sxz + syz * syz)
    strength = plastic_params[0] + plastic_params[1] * jnp.maximum(-mean, 0.0)
    factor = strength / jnp.maximum(tau, strength)
    factor = jnp.where(fault_mask == 1, factor, jnp.ones((), jnp.float32))
    return (
        mean + dxx * factor,
        mean + dyy * factor,
        mean + dzz * factor,
        sxy * factor,
        sxz * factor,
        syz * factor,
    )


def with_before(field, face, axis):
    rest = lax.slice_in_dim(field, 0, field.shape[axis] - 1, axis=axis)
    return jnp.concatenate([face, rest], axis=axis)


def with_after(field, face, axis):
    rest = lax.slice_in_dim(field, 1, field.shape[axis], axis=axis)
    return jnp.concatenate([rest, face], axis=axis)


def pick_slots(quarters, wanted):
    slots = jnp.zeros((wanted.shape[0], quarters.shape[0], quarters.shape[2]), jnp.float32)
    for quarter in range(quarters.shape[1]):
        keep = wanted[:, quarter][:, None, None]
        slots = slots + jnp.where(keep, quarters[None, :, quarter, :], jnp.zeros((), jnp.float32))
    return slots


def assemble(received, owned, ranks, n_grp):
    pieces = []
    for quarter in range(n_grp):
        keep = (owned & (ranks % n_grp == quarter))[:, None, None]
        pieces.append(jnp.sum(jnp.where(keep, received, jnp.zeros((), jnp.float32)), axis=0))
    whole = jnp.stack(pieces, axis=1)
    return whole.reshape(whole.shape[0], whole.shape[1] * whole.shape[2])


def seafloor_to_ocean(slab):
    n_grp = lax.axis_size("grp")
    n_gy = lax.axis_size("gy")
    group = lax.axis_index("grp")
    column = lax.axis_index("gy")
    width = slab.shape[1] // n_grp
    quarter_ids = jnp.arange(n_grp)
    quarters = slab.reshape(slab.shape[0], n_grp, width)
    ranks = jnp.arange(n_grp * n_gy)
    owned = (ranks // n_grp == column) & (group == 0)
    wanted = owned[:, None] & ((ranks % n_grp)[:, None] == quarter_ids[None, :])
    received = lax.all_to_all(
        pick_slots(quarters, wanted), ("grp", "gy"), split_axis=0, concat_axis=0, tiled=True
    )
    return jnp.sum(received, axis=0)


def pressure_to_solid(bottom):
    n_grp = lax.axis_size("grp")
    n_gy = lax.axis_size("gy")
    group = lax.axis_index("grp")
    column = lax.axis_index("gy")
    rank = group * n_gy + column
    targets = jnp.arange(n_grp * n_gy) == rank // n_grp
    slots = jnp.where(targets[:, None, None], bottom[None], jnp.zeros((), jnp.float32))
    received = lax.all_to_all(slots, ("grp", "gy"), split_axis=0, concat_axis=0, tiled=True)
    ranks = jnp.arange(n_grp * n_gy)
    owned = (ranks // n_grp == column) & (group == 0)
    return assemble(received, owned, ranks, n_grp)


def body(
    solid_velocity,
    solid_stress,
    ocean_pressure,
    ocean_velocity,
    surface,
    materials,
    region_ids,
    fault_mask,
    plastic_params,
):
    is_top = (lax.axis_index("grp") == 0).astype(jnp.float32)
    lame_lambda = lookup(region_ids, materials[0])
    shear_modulus = lookup(region_ids, materials[1])
    buoy = lookup(region_ids, materials[2])
    vx, vy, vz = (solid_velocity[0], solid_velocity[1], solid_velocity[2])
    stress_xx_part, stress_yy_part, stress_zz_part, sxy, sxz, syz = [
        solid_stress[k] for k in range(6)
    ]
    press = ocean_pressure
    flow_x, flow_y, lift = (ocean_velocity[0], ocean_velocity[1], ocean_velocity[2])
    height = surface
    for _ in range(STEPS):
        load = pressure_to_solid(press[0]) * is_top
        face_x = from_behind(
            jnp.stack([stress_xx_part[:, -1:, :], sxy[:, -1:, :], sxz[:, -1:, :]]), "gx", 1
        )
        face_y = from_behind(
            jnp.stack([sxy[:, :, -1:], stress_yy_part[:, :, -1:], syz[:, :, -1:]]), "gy", 1
        )
        face_z = from_behind(jnp.stack([sxz[-1:], syz[-1:], stress_zz_part[-1:]]), "grp", 1)
        szz_face = face_z[2] - load[None]
        div_x = (
            stress_xx_part
            - with_before(stress_xx_part, face_x[0], 1)
            + (sxy - with_before(sxy, face_y[0], 2))
            + (sxz - with_before(sxz, face_z[0], 0))
        )
        div_y = (
            sxy
            - with_before(sxy, face_x[1], 1)
            + (stress_yy_part - with_before(stress_yy_part, face_y[1], 2))
            + (syz - with_before(syz, face_z[1], 0))
        )
        div_z = (
            sxz
            - with_before(sxz, face_x[2], 1)
            + (syz - with_before(syz, face_y[2], 2))
            + (stress_zz_part - with_before(stress_zz_part, szz_face, 0))
        )
        vx = vx + courant_number * buoy * div_x
        vy = vy + courant_number * buoy * div_y
        vz = vz + courant_number * buoy * div_z
        motion = jnp.stack([vx, vy, vz])
        next_x = from_behind(motion[:, :, :1, :], "gx", -1)
        next_y = from_behind(motion[:, :, :, :1], "gy", -1)
        next_z = from_behind(motion[:, :1], "grp", -1)
        gradient_xx_part, gxy, gxz = (
            with_after(vx, next_x[0], 1) - vx,
            with_after(vx, next_y[0], 2) - vx,
            with_after(vx, next_z[0], 0) - vx,
        )
        gyx, gradient_yy_part, gyz = (
            with_after(vy, next_x[1], 1) - vy,
            with_after(vy, next_y[1], 2) - vy,
            with_after(vy, next_z[1], 0) - vy,
        )
        gzx, gzy, gradient_zz_part = (
            with_after(vz, next_x[2], 1) - vz,
            with_after(vz, next_y[2], 2) - vz,
            with_after(vz, next_z[2], 0) - vz,
        )
        dilatation = gradient_xx_part + gradient_yy_part + gradient_zz_part
        stress_xx_part = stress_xx_part + courant_number * (
            lame_lambda * dilatation + 2.0 * shear_modulus * gradient_xx_part
        )
        stress_yy_part = stress_yy_part + courant_number * (
            lame_lambda * dilatation + 2.0 * shear_modulus * gradient_yy_part
        )
        stress_zz_part = stress_zz_part + courant_number * (
            lame_lambda * dilatation + 2.0 * shear_modulus * gradient_zz_part
        )
        sxy = sxy + courant_number * shear_modulus * (gxy + gyx)
        sxz = sxz + courant_number * shear_modulus * (gxz + gzx)
        syz = syz + courant_number * shear_modulus * (gyz + gzy)
        stress_xx_part, stress_yy_part, stress_zz_part, sxy, sxz, syz = yield_cap(
            stress_xx_part,
            stress_yy_part,
            stress_zz_part,
            sxy,
            sxz,
            syz,
            fault_mask,
            plastic_params,
        )
        floor_lift = seafloor_to_ocean(vz[0])
        press_x = from_behind(press[:, :1, :], "gx", -1)
        press_y = from_behind(press[:, :, :1], ("grp", "gy"), -1)
        flow_x = flow_x - ocean_step * (with_after(press, press_x, 1) - press)
        flow_y = flow_y - ocean_step * (with_after(press, press_y, 2) - press)
        above = jnp.concatenate([press[1:], (gravity_term * height)[None]], axis=0)
        lift = lift - vertical_step * (above - press)
        lift_below = jnp.concatenate([floor_lift[None], lift[:-1]], axis=0)
        flow_prev_x = from_behind(flow_x[:, -1:, :], "gx", 1)
        flow_prev_y = from_behind(flow_y[:, :, -1:], ("grp", "gy"), 1)
        spread = (
            flow_x
            - with_before(flow_x, flow_prev_x, 1)
            + (flow_y - with_before(flow_y, flow_prev_y, 2))
        )
        press = press - ocean_step * spread - vertical_step * (lift - lift_below)
        height = height + surface_step * lift[-1]
    return (
        jnp.stack([vx, vy, vz]),
        jnp.stack([stress_xx_part, stress_yy_part, stress_zz_part, sxy, sxz, syz]),
        press,
        jnp.stack([flow_x, flow_y, lift]),
        height,
    )


FIELDS = 11
REGION, FAULT = 9, 10
SZZ, SXZ, SYZ = 5, 7, 8
BASE = 4 * FIELDS


def row_of(shape):
    return lax.broadcasted_iota(jnp.int32, shape, len(shape) - 2)


def lane_of(shape):
    return lax.broadcasted_iota(jnp.int32, shape, len(shape) - 1)


def turn(tile, shift, axis):
    if isinstance(shift, int):
        shift %= tile.shape[axis]
        return tile if shift == 0 else pltpu.roll(tile, shift, axis)
    return pltpu.roll(tile, shift, axis)


def lanes_at(c):
    return slice(c * 128, c * 128 + 128)


def rows_kernel(
    v, s, region, fault, p, u, h, materials_raw, plastic_raw,
    cells, sea, first, last, up, down, table, region_in, fault_in, materials, plastic, sems,
):
    layers, n, width = s.shape[1:]
    depth = p.shape[0]
    inner = (pl.ds(2, layers), pl.ds(0, n), pl.ds(0, width))
    copies = [
        pltpu.make_async_copy(v, cells.at[(pl.ds(0, 3), *inner)], sems.at[0]),
        pltpu.make_async_copy(s, cells.at[(pl.ds(3, 6), *inner)], sems.at[1]),
        pltpu.make_async_copy(region, region_in, sems.at[2]),
        pltpu.make_async_copy(fault, fault_in, sems.at[3]),
        pltpu.make_async_copy(p, sea.at[pl.ds(0, depth)], sems.at[4]),
        pltpu.make_async_copy(h, sea.at[4 * depth], sems.at[5]),
        pltpu.make_async_copy(materials_raw, materials, sems.at[9]),
        pltpu.make_async_copy(plastic_raw, plastic, sems.at[10]),
    ]
    copies += [
        pltpu.make_async_copy(u.at[k], sea.at[pl.ds((k + 1) * depth, depth)], sems.at[6 + k])
        for k in range(3)
    ]
    for copy in copies:
        copy.start()
    for copy in copies:
        copy.wait()
    for z in range(layers):
        cells[REGION, z + 2, 0:n, 0:width] = region_in[z].astype(jnp.float32) + 1.0
        cells[FAULT, z + 2, 0:n, 0:width] = fault_in[z].astype(jnp.float32)
    row = row_of((8, width))

    def pack(f, carry):
        a = b = jnp.zeros((8, width), jnp.float32)
        for z in range(layers):
            mine = row // 2 == z
            a = jnp.where(mine, turn(cells[f, z + 2, 0:8, 0:width], 2 * z, 0), a)
            b = jnp.where(mine, turn(cells[f, z + 2, n - 8 : n, 0:width], 2 * z + 2, 0), b)
        first[f] = a
        last[f] = b
        down[3 + f] = cells[f, layers + 1, 0:n, 0:width]
        return carry

    walk(0, FIELDS, pack, 0)

    def lift_up(f, carry):
        up[2 * f] = cells[f, 2, 0:n, 0:width]
        up[2 * f + 1] = cells[f, 3, 0:n, 0:width]
        return carry

    walk(0, FAULT, lift_up, 0)
    up[2 * FAULT] = cells[FAULT, 2, 0:n, 0:width]
    for i, f in enumerate((SZZ, SXZ, SYZ)):
        down[i] = cells[f, layers, 0:n, 0:width]
    w = sea.shape[2]
    row = row_of((8, w))
    planes = 4 * depth + 1
    per = width // w
    for t in range((first.shape[0] - FIELDS) * per):
        a = b = jnp.zeros((8, w), jnp.float32)
        for q in range(4):
            if 4 * t + q < planes:
                mine = row // 2 == q
                a = jnp.where(mine, turn(sea[4 * t + q, 0:8], 2 * q, 0), a)
                b = jnp.where(mine, turn(sea[4 * t + q, n - 8 : n], 2 * q + 2, 0), b)
        first[FIELDS + t // per, :, lanes_at(t % per)] = a
        last[FIELDS + t // per, :, lanes_at(t % per)] = b
    shape = table.shape[1:]
    lane = lane_of(shape)
    for k in range(3):
        tile = jnp.zeros(shape, jnp.float32)
        for r in range(REGIONS):
            tile = jnp.where(lane == r + 1, courant_number * materials[k, r], tile)
        table[k] = tile
    for k in range(2):
        table[3 + k] = jnp.full(shape, plastic[k])


def tables(table):
    return [table[k, 0:8] for k in range(3)]


def look(cells, stuff, table, slot, rows, lanes):
    for r in range(rows.start, rows.stop, 8):
        at = slice(r, r + 8)
        for c in range(lanes.start, lanes.stop, 128):
            lane = slice(c, c + 128)
            index = cells[REGION, slot, at, lane].astype(jnp.int32)
            for k in range(3):
                stuff[k, slot, at, lane] = jnp.take_along_axis(table[k], index, axis=1)


def columns_kernel(table_ref, cells, sea, stuff, solid_out, first_out, last_out):
    here = lax.axis_index("gy") == 0
    layers = cells.shape[1] - 4
    n = solid_out.shape[0]
    width = cells.shape[3] - 128
    lane = lane_of((n, 128)) // 2
    spot = jnp.where(here, (lane + 1) % 64, lane)

    def pack(f, total):
        for z in range(layers):
            tile = jnp.where(
                here,
                cells[f, z + 2, 0:n, width - 128 : width],
                cells[f, z + 2, 0:n, 0:128],
            )
            j = f * layers + z
            total = jnp.where(spot == j, turn(tile, 2 * j, 1), total)
        return total

    zero = jnp.zeros((n, 128), jnp.float32)
    total = walk(0, FIELDS, pack, zero)
    solid_out[...] = jnp.where(here, turn(total, 2, 1), total)

    def pack_sea(j, carry):
        a, b = carry
        tile = sea[j]
        rolled = turn(tile, 2 * j, 1)
        a = jnp.where(lane == j, rolled, a)
        b = jnp.where((lane + 1) % 64 == j, rolled, b)
        return a, b

    a, b = walk(0, sea.shape[0], pack_sea, (zero, zero))
    first_out[...] = a
    last_out[...] = turn(b, 2, 1)
    table = tables(table_ref)

    def find(z, carry):
        look(cells, stuff, table, z, slice(0, n), slice(0, width))
        return carry

    walk(2, layers + 2, find, 0)


def rim(after, before, slot):
    row = row_of(after.shape)
    tile = jnp.where(row < 2, turn(after, -2 * slot, 0), 0.0)
    return jnp.where(row >= 6, turn(before, 6 - 2 * slot, 0), tile)


def sea_rim(after, before, plane, per):
    t, q = plane // 4, plane % 4
    lanes = lanes_at(t % per)
    k = FIELDS + t // per
    return rim(after[k, :, lanes], before[k, :, lanes], q)


def before_x(tile):
    return turn(tile, 1, 0)


def after_x(tile):
    return turn(tile, -1, 0)


def sides_kernel(after, before, solid, first, last, sea, out):
    here = lax.axis_index("gy") == 0
    n = solid.shape[0]
    layers = after.shape[1] // 2
    width = after.shape[2]
    per = width // 128
    lane = lane_of((8, 128)) // 2
    depth = sea.shape[0] // 4
    zero = jnp.zeros((8, 128), jnp.float32)
    spot = jnp.where(here, (lane + 1) % 64, lane)

    def pack(f, total):
        a = jnp.where(here, after[f, :, width - 128 :], after[f, :, :128])
        b = jnp.where(here, before[f, :, width - 128 :], before[f, :, :128])
        for z in range(layers):
            j = f * layers + z
            total = jnp.where(spot == j, turn(rim(a, b, z), 2 * j, 1), total)
        return total

    out[0, :n] = solid[...]
    total = walk(0, FIELDS, pack, zero)
    out[0, n:] = jnp.where(here, turn(total, 2, 1), total)

    def pack_sea(k, carry):
        a, b = carry
        for i in range(4 * per):
            j = 4 * per * k + i
            x = after[FIELDS + k, :, lanes_at(i // 4)]
            y = before[FIELDS + k, :, lanes_at(i // 4)]
            rolled = turn(rim(x, y, i % 4), 2 * j, 1)
            a = jnp.where(lane == j, rolled, a)
            b = jnp.where((lane + 1) % 64 == j, rolled, b)
        return a, b

    out[1, :n] = first[...]
    out[2, :n] = last[...]
    a, b = walk(0, after.shape[0] - FIELDS, pack_sea, (zero, zero))
    out[1, n:] = a
    out[2, n:] = turn(b, 2, 1)

    def grown(plane):
        return jnp.concatenate([sea[plane], sea_rim(after, before, plane, per)], axis=0)

    row = row_of((n + 8, 128))
    p0, p1 = grown(0), grown(1)
    ux = grown(depth) - ocean_step * (after_x(p0) - p0)
    ux = jnp.where((row == n + 7) & (lax.axis_index("gx") == 0), 0.0, ux)
    w = grown(3 * depth) - vertical_step * (p1 - p0)
    out[3] = p0
    out[4] = grown(2 * depth)
    out[5] = p0 - ocean_step * (ux - before_x(ux)) - vertical_step * w


def rims_kernel(table_ref, after, before, cells_in, stuff_in, cells, stuff):
    layers = after.shape[1] // 2
    width = after.shape[2]
    tall = cells.shape[2]
    n = tall - 8

    def fill(f, carry):
        for c in range(width // 128):
            a, b = after[f, :, lanes_at(c)], before[f, :, lanes_at(c)]
            for z in range(layers):
                cells[f, z + 2, n:tall, lanes_at(c)] = rim(a, b, z)
        return carry

    walk(0, FIELDS, fill, 0)
    table = tables(table_ref)

    def find(z, carry):
        look(cells, stuff, table, z, slice(n, tall), slice(0, width))
        return carry

    walk(2, layers + 2, find, 0)


def frames_kernel(after, before, mine, other, up, down, deep):
    row = row_of((8, 128))

    def pack(f, carry):
        for c in range(after.shape[2] // 128):
            a, b = after[f, :, lanes_at(c)], before[f, :, lanes_at(c)]
            up[4 * f + c] = jnp.where(row < 4, a, turn(b, 4, 0))
            down[4 * f + c] = jnp.where(row < 4, turn(a, 4, 0), b)
        return carry

    walk(0, FIELDS, pack, 0)
    for i in range(3):
        rows = slice(8 * i, 8 * i + 8)
        up[BASE + i] = other[0, rows]
        down[BASE + i] = other[0, rows]
        up[BASE + 3 + i] = other[1, rows]
        down[BASE + 3 + i] = other[2, rows]
        for k in range(3):
            for m, source in enumerate((mine, other)):
                tile = source[3 + k, rows]
                place = 9 * m + 3 * k + i
                up[BASE + 6 + place] = tile
                deep[place] = tile


def three(ref, at):
    return jnp.concatenate([ref[at], ref[at + 1], ref[at + 2]], axis=0)


def side_ready(packed, here, lane):
    mask = (here & (lane < 2)) | (jnp.logical_not(here) & (lane >= 126))
    return jnp.where(here, packed, turn(packed, 126, 1)), mask


def side_tile(packed, j):
    return jnp.where(packed[1], turn(packed[0], 128 - 2 * j, 1), 0.0)


def before_y(tile, neighbour):
    return turn(jnp.where(lane_of(tile.shape) == 127, neighbour, tile), 1, 1)


def after_y(tile, neighbour):
    return turn(jnp.where(lane_of(tile.shape) == 0, neighbour, tile), -1, 1)


def velocity(cells, stuff, z, lifts=None):
    chunks = cells.shape[3] // 128
    for c in range(chunks):
        lanes, behind = lanes_at(c), lanes_at((c - 1) % chunks)
        xx, yy, zz, xy, xz, yz = [cells[3 + k, z, :, lanes] for k in range(6)]
        gain = stuff[2, z, :, lanes]
        div_z = (
            (xz - before_x(xz))
            + (yz - before_y(yz, cells[SYZ, z, :, behind]))
            + (zz - cells[SZZ, z - 1, :, lanes])
        )
        vz = cells[2, z, :, lanes] + gain * div_z
        if lifts is not None:
            lifts[:, lanes] = vz
            continue
        div_x = (
            (xx - before_x(xx))
            + (xy - before_y(xy, cells[6, z, :, behind]))
            + (xz - cells[SXZ, z - 1, :, lanes])
        )
        div_y = (
            (xy - before_x(xy))
            + (yy - before_y(yy, cells[4, z, :, behind]))
            + (yz - cells[SYZ, z - 1, :, lanes])
        )
        cells[0, z, :, lanes] = cells[0, z, :, lanes] + gain * div_x
        cells[1, z, :, lanes] = cells[1, z, :, lanes] + gain * div_y
        cells[2, z, :, lanes] = vz


def stress(cells, stuff, plastic, z, out=None):
    chunks = cells.shape[3] // 128
    rows = cells.shape[2] if out is None else out.shape[2]
    keep = slice(0, rows)
    cohesion, friction = plastic[3, keep], plastic[4, keep]
    for c in range(chunks if out is None else chunks - 1):
        lanes, ahead = lanes_at(c), lanes_at((c + 1) % chunks)
        vx, vy, vz = [cells[k, z, :, lanes] for k in range(3)]
        kx, ky, kz = vx[keep], vy[keep], vz[keep]
        nx, ny, nz = [cells[k, z, keep, ahead] for k in range(3)]
        bx, by, bz = [cells[k, z + 1, keep, lanes] for k in range(3)]
        gxx, gxy, gxz = after_x(vx)[keep] - kx, after_y(kx, nx) - kx, bx - kx
        gyx, gyy, gyz = after_x(vy)[keep] - ky, after_y(ky, ny) - ky, by - ky
        gzx, gzy, gzz = after_x(vz)[keep] - kz, after_y(kz, nz) - kz, bz - kz
        lam, mu = stuff[0, z, keep, lanes], stuff[1, z, keep, lanes]
        xx, yy, zz, xy, xz, yz = [cells[3 + k, z, keep, lanes] for k in range(6)]
        swell = lam * (gxx + gyy + gzz)
        two = mu + mu
        xx = xx + (swell + two * gxx)
        yy = yy + (swell + two * gyy)
        zz = zz + (swell + two * gzz)
        xy = xy + mu * (gxy + gyx)
        xz = xz + mu * (gxz + gzx)
        yz = yz + mu * (gyz + gzy)
        mean = (xx + yy + zz) * (1.0 / 3.0)
        dxx, dyy, dzz = xx - mean, yy - mean, zz - mean
        square = 0.5 * (dxx * dxx + dyy * dyy + dzz * dzz) + xy * xy + xz * xz + yz * yz
        strength = cohesion + friction * jnp.maximum(-mean, 0.0)
        factor = jnp.minimum(strength * lax.rsqrt(square), 1.0)
        factor = jnp.where(cells[FAULT, z, keep, lanes] == 1.0, factor, 1.0)
        result = (
            mean + dxx * factor,
            mean + dyy * factor,
            mean + dzz * factor,
            xy * factor,
            xz * factor,
            yz * factor,
        )
        for k, tile in enumerate(result):
            if out is None:
                cells[3 + k, z, :, lanes] = tile
            else:
                out[k, z - 2, :, lanes] = tile


def each(first, last, step):
    for z in range(first, last):
        step(z)


def walk(first, last, step, carry):
    for z in range(first, last):
        carry = step(z, carry)
    return carry


def early_kernel(table_ref, low, high, side, cells_in, stuff_in, cells, stuff):
    here = lax.axis_index("gy") == 0
    layers = cells.shape[1] - 4
    tall, wide = cells.shape[2:]
    n, width = tall - 8, wide - 128
    lane = lane_of((tall, 128))
    packed = side_ready(side[0], here, lane)

    def fill(f):
        for z in range(layers):
            cells[f, z + 2, :, width:wide] = side_tile(packed, f * layers + z)
        cells[f, 1, 0:n, 0:width] = low[3 + f]
        cells[f, layers + 2, 0:n, 0:width] = high[2 * f]

    each(0, FIELDS, fill)

    def fill_last(f):
        cells[f, layers + 3, 0:n, 0:width] = high[2 * f + 1]

    each(0, FAULT, fill_last)
    for i, f in enumerate((SZZ, SXZ, SYZ)):
        cells[f, 0, 0:n, 0:width] = low[i]
    table = tables(table_ref)
    each(2, layers + 2, lambda z: look(cells, stuff, table, z, slice(0, tall), slice(width, wide)))
    each(3, layers + 2, lambda z: velocity(cells, stuff, z))
    each(3, layers + 1, lambda z: stress(cells, stuff, table_ref, z))
    each(1, 2, lambda z: look(cells, stuff, table, z, slice(0, n), slice(0, width)))
    each(
        layers + 2,
        layers + 4,
        lambda z: look(cells, stuff, table, z, slice(0, n), slice(0, width)),
    )


def ghost_rim(cells, f, slot, place, packed, j, frame, top):
    tall, wide = cells.shape[2:]
    n, width = tall - 8, wide - 128
    row = row_of((8, 128))
    cells[f, slot, :, width:wide] = side_tile(packed, j)
    for c in range(width // 128):
        source = frame[4 * f + c]
        tile = jnp.where(row < 2, turn(source, -2 * place, 0), 0.0)
        tile = jnp.where(row >= 6, turn(source, 2 - 2 * place, 0), tile)
        if top is not None:
            tile = jnp.where(top, 0.0, tile)
        cells[f, slot, n:tall, lanes_at(c)] = tile


def find_rim(cells, stuff, table, slot):
    tall, wide = cells.shape[2:]
    n, width = tall - 8, wide - 128
    look(cells, stuff, table, slot, slice(0, tall), slice(width, wide))
    look(cells, stuff, table, slot, slice(n, tall), slice(0, width))


def floor_kernel(
    table_ref, side, mine, frame_low, frame_high, two_up, three_up,
    cells_in, stuff_in, cells, stuff, lift_out, sea_state,
):
    top = lax.axis_index("grp") == 0
    here = lax.axis_index("gy") == 0
    layers = cells.shape[1] - 4
    tall, wide = cells.shape[2:]
    width = wide - 128
    chunks = width // 128
    lane = lane_of((tall, 128))
    side_low = side_ready(jnp.where(top, 0.0, three(frame_low, BASE)), here, lane)

    def fill(f):
        ghost_rim(cells, f, 1, 1, side_low, f * layers + layers - 1, frame_low, top)

    each(0, FIELDS, fill)
    table = tables(table_ref)
    find_rim(cells, stuff, table, 1)

    def sea_tile(k, r):
        m, odd = r // 2, r % 2
        if m == 0:
            a, b = mine[3 + k], side[3 + k]
        else:
            ref = (None, frame_high, two_up, three_up)[m]
            base = BASE + 6 if m == 1 else 0
            a, b = three(ref, base + 3 * k), three(ref, base + 9 + 3 * k)
        return jnp.where(here, b, a) if odd else jnp.where(here, a, b)

    for k in range(3):
        for c in range(chunks):
            sea_state[k, :, lanes_at(c)] = jnp.where(
                here, sea_tile(k, c), sea_tile(k, chunks + c)
            )
        tile = jnp.where(here & (lane < 2), sea_tile(k, chunks), 0.0)
        sea_state[k, :, width:wide] = jnp.where(
            jnp.logical_not(here) & (lane >= 126), sea_tile(k, chunks - 1), tile
        )
    for c in range(chunks + 1):
        lanes = lanes_at(c)
        cells[SZZ, 1, :, lanes] = jnp.where(top, -sea_state[0, :, lanes], cells[SZZ, 1, :, lanes])
        p0 = sea_state[0, :, lanes]
        uy = sea_state[1, :, lanes] - ocean_step * (
            after_y(p0, sea_state[0, :, lanes_at((c + 1) % (chunks + 1))]) - p0
        )
        sea_state[1, :, lanes] = jnp.where(cells[REGION, 2, :, lanes] > 0.5, uy, 0.0)
    each(2, 3, lambda z: velocity(cells, stuff, z))
    each(2, 3, lambda z: stress(cells, stuff, table_ref, z))
    for c in range(chunks + 1):
        lanes = lanes_at(c)
        uy = sea_state[1, :, lanes]
        lift = cells[2, 2, :, lanes]
        press = (
            sea_state[2, :, lanes]
            - ocean_step * (uy - before_y(uy, sea_state[1, :, lanes_at((c - 1) % (chunks + 1))]))
            + vertical_step * lift
        )
        sea_state[3, :, lanes] = lift
        cells[SZZ, 1, :, lanes] = jnp.where(top, -press, cells[SZZ, 1, :, lanes])
    velocity(cells, stuff, 2, sea_state.at[4])
    for c in range(chunks):
        ahead = sea_state[3, :, lanes_at(c + 1)]
        behind = sea_state[3, :, lanes_at((c - 1) % (chunks + 1))]
        lift_out[c, 0] = sea_state[3, :, lanes_at(c)]
        lift_out[c, 1] = jnp.where(lane == 0, ahead, jnp.where(lane == 127, behind, 0.0))
        lift_out[c, 2] = sea_state[4, :, lanes_at(c)]


def solid_kernel(
    table_ref, frame_low, frame_high, cells_in, stuff_in,
    cells, stuff, v_out, s_out,
):
    top = lax.axis_index("grp") == 0
    here = lax.axis_index("gy") == 0
    layers = cells.shape[1] - 4
    tall, wide = cells.shape[2:]
    n, width = tall - 8, wide - 128
    lane = lane_of((tall, 128))
    side_low = side_ready(jnp.where(top, 0.0, three(frame_low, BASE)), here, lane)
    side_high = side_ready(three(frame_high, BASE), here, lane)

    def fill_high(f):
        ghost_rim(cells, f, layers + 2, 0, side_high, f * layers, frame_high, None)

    def fill_last(f):
        ghost_rim(cells, f, layers + 3, 1, side_high, f * layers + 1, frame_high, None)

    each(0, FIELDS, fill_high)
    each(0, FAULT, fill_last)
    for f in (SZZ, SXZ, SYZ):
        ghost_rim(cells, f, 0, 0, side_low, f * layers + layers - 2, frame_low, top)
    table = tables(table_ref)
    each(layers + 2, layers + 4, lambda z: find_rim(cells, stuff, table, z))
    each(layers + 2, layers + 4, lambda z: velocity(cells, stuff, z))

    @pl.when(jnp.logical_not(top))
    def _():
        velocity(cells, stuff, 1)
        stress(cells, stuff, table_ref, 1)

    each(layers + 1, layers + 3, lambda z: stress(cells, stuff, table_ref, z))
    each(2, layers + 3, lambda z: velocity(cells, stuff, z))
    for k in range(3):
        for z in range(layers):
            v_out[k, z] = cells[k, z + 2, 0:n, 0:width]
    each(2, layers + 2, lambda z: stress(cells, stuff, table_ref, z, s_out))


def ocean_kernel(
    sea, after, before, side, frame_low, frame_high, la, lb, lc, ld,
    p_out, u_out, h_out, ext,
):
    here = lax.axis_index("gy") == 0
    group, groups = lax.axis_index("grp"), lax.axis_size("grp")
    column, columns = lax.axis_index("gy"), lax.axis_size("gy")
    strike, strikes = lax.axis_index("gx"), lax.axis_size("gx")
    rank = group * columns + column
    layers, n, w = p_out.shape
    tall, wide = n + 8, 2 * w
    per = after.shape[2] // 128
    row, lane = row_of((tall, wide)), lane_of((tall, wide))
    small = lane_of((tall, w))
    inside = jnp.logical_not((row == n) & (strike == strikes - 1))
    inside &= jnp.logical_not((row == tall - 1) & (strike == 0))
    inside &= jnp.logical_not((lane == w) & (rank == groups * columns - 1))
    inside &= jnp.logical_not((lane == wide - 1) & (rank == 0))
    at = BASE + 3
    ahead = jnp.where(here, side[1], three(frame_high, at))
    behind = jnp.where(here, jnp.where(group == 0, 0.0, three(frame_low, at)), side[2])

    def grown(plane):
        tile = jnp.concatenate([sea[plane], sea_rim(after, before, plane, per)], axis=0)
        edge = jnp.where(small < 2, turn(ahead, -2 * plane, 1), 0.0)
        edge = jnp.where(small >= 126, turn(behind, 126 - 2 * plane, 1), edge)
        return jnp.concatenate([tile, edge], axis=1)

    for j in range(4 * layers + 1):
        ext[j] = grown(j)

    def moved(press, flow, axis):
        flow = flow - ocean_step * (turn(press, -1, axis) - press)
        return jnp.where(inside, flow, 0.0)

    for step in range(STEPS):
        final = step == STEPS - 1
        if step == 0:
            below = jnp.concatenate(
                [la[0] + lb[0] + lc[0] + ld[0], la[1] + lb[1] + lc[1] + ld[1]], axis=1
            )
        else:
            below = jnp.concatenate(
                [la[2] + lb[2] + lc[2] + ld[2], jnp.zeros((tall, w), jnp.float32)], axis=1
            )
        height = ext[4 * layers]
        for k in range(layers):
            press = ext[k]
            ux = moved(press, ext[layers + k], 0)
            uy = moved(press, ext[2 * layers + k], 1)
            above = gravity_term * height if k == layers - 1 else ext[k + 1]
            lift = ext[3 * layers + k] - vertical_step * (above - press)
            spread = ux - turn(ux, 1, 0) + (uy - turn(uy, 1, 1))
            press = press - ocean_step * spread - vertical_step * (lift - below)
            below = lift
            if final:
                p_out[k] = press[:n, :w]
                u_out[0, k] = ux[:n, :w]
                u_out[1, k] = uy[:n, :w]
                u_out[2, k] = lift[:n, :w]
            else:
                ext[k] = jnp.where(inside, press, 0.0)
                ext[layers + k] = ux
                ext[2 * layers + k] = uy
                ext[3 * layers + k] = lift
        height = height + surface_step * below
        if final:
            h_out[...] = height[:n, :w]
        else:
            ext[4 * layers] = height


def call(kernel, shapes, inputs, scratch=(), smem=0, alias=None, raw=False, work=0):
    if raw:
        inputs = [pltpu.with_memory_space_constraint(x, pltpu.HBM) for x in inputs]
    vmem = pl.BlockSpec(memory_space=pltpu.VMEM)
    kept = pl.BlockSpec(memory_space=pltpu.HBM) if raw else vmem
    specs = [pl.BlockSpec(memory_space=pltpu.SMEM)] * smem + [kept] * (len(inputs) - smem)
    outs = [jax.ShapeDtypeStruct(shape, jnp.float32) for shape in shapes]
    return pl.pallas_call(
        kernel,
        out_shape=outs,
        in_specs=specs,
        out_specs=[vmem] * len(outs),
        scratch_shapes=list(scratch),
        input_output_aliases=alias or {},
        compiler_params=pltpu.CompilerParams(vmem_limit_bytes=30 * 1024 * 1024),
        cost_estimate=pl.CostEstimate(flops=work, bytes_accessed=work, transcendentals=0),
    )(*inputs)


def fast_body(*arrays):
    return relayed(*arrays)


def along(count, steps):
    return [(i, i + steps) for i in range(count) if 0 <= i + steps < count]


def relayed(v, s, p, u, h, materials, region, fault, plastic):
    layers, n, width = s.shape[1:]
    depth, _, w = p.shape
    tall, wide = n + 8, width + 128
    planes = 4 * depth + 1
    slabs = FIELDS + -(-planes // (4 * (width // w)))
    n_grp, n_gy = lax.axis_size("grp"), lax.axis_size("gy")
    held = (FIELDS, layers + 4, tall, wide)
    coded = (3, layers + 4, tall, wide)
    cells, sea, first, last, up, down, table = call(
        rows_kernel,
        [
            held,
            (planes, n, w),
            (slabs, 8, width),
            (slabs, 8, width),
            (2 * FIELDS - 1, n, width),
            (FIELDS + 3, n, width),
            (5, tall, 128),
        ],
        (v, s, region, fault, p, u, h, materials, plastic),
        scratch=[
            pltpu.VMEM((layers, n, width), jnp.int32),
            pltpu.VMEM((layers, n, width), jnp.int32),
            pltpu.SMEM(materials.shape, jnp.float32),
            pltpu.SMEM(plastic.shape, jnp.float32),
            pltpu.SemaphoreType.DMA((11,)),
        ],
        raw=True,
    )
    n_gx = lax.axis_size("gx")
    after = lax.ppermute(first, "gx", along(n_gx, -1))
    before = lax.ppermute(last, "gx", along(n_gx, 1))
    high = lax.ppermute(up, "grp", along(n_grp, -1))
    low = lax.ppermute(down, "grp", along(n_grp, 1))
    stuff, *own = call(
        columns_kernel, [coded] + [(n, 128)] * 3, (table, cells, sea),
        work=1 << 20,
    )
    (mine,) = call(sides_kernel, [(6, tall, 128)], (after, before, *own, sea))
    side = lax.ppermute(mine, "gy", [(i, n_gy - 1 - i) for i in range(n_gy)])
    cells, stuff = call(
        rims_kernel, [held, coded], (table, after, before, cells, stuff),
        alias={3: 0, 4: 1}, work=1 << 20,
    )
    frame_up, frame_down, deep = call(
        frames_kernel,
        [(BASE + 24, 8, 128), (BASE + 6, 8, 128), (18, 8, 128)],
        (after, before, mine, side),
    )
    frame_high = lax.ppermute(frame_up, "grp", along(n_grp, -1))
    frame_low = lax.ppermute(frame_down, "grp", along(n_grp, 1))
    two_up = lax.ppermute(deep, "grp", [(2, 0)])
    three_up = lax.ppermute(deep, "grp", [(3, 0)])
    cells, stuff = call(
        early_kernel, [held, coded], (table, low, high, side, cells, stuff),
        alias={4: 0, 5: 1}, work=1 << 22,
    )
    cells, stuff, lift = call(
        floor_kernel,
        [held, coded, (width // w, 3, tall, w)],
        (
            table, side, mine, frame_low, frame_high, two_up, three_up, cells, stuff,
        ),
        scratch=[pltpu.VMEM((5, tall, wide), jnp.float32)],
        alias={7: 0, 8: 1},
    )
    lifts = [
        lax.ppermute(
            lift[k], ("grp", "gy"), [(r // n_grp, r) for r in range(k, n_grp * n_gy, n_grp)]
        )
        for k in range(n_grp)
    ]
    cells, stuff, v_out, s_out = call(
        solid_kernel,
        [held, coded, v.shape, s.shape],
        (table, frame_low, frame_high, cells, stuff),
        alias={3: 0, 4: 1},
        work=1 << 23,
    )
    p_out, u_out, h_out = call(
        ocean_kernel,
        [p.shape, u.shape, h.shape],
        (sea, after, before, side, frame_low, frame_high, *lifts),
        scratch=[pltpu.VMEM((planes, tall, 2 * w), jnp.float32)],
    )
    return v_out, s_out, p_out, u_out, h_out


def solution(mesh):
    placed = (
        P(None, "grp", "gx", "gy"),
        P(None, "grp", "gx", "gy"),
        P(None, "gx", ("grp", "gy")),
        P(None, None, "gx", ("grp", "gy")),
        P("gx", ("grp", "gy")),
        P(),
        P("grp", "gx", "gy"),
        P("grp", "gx", "gy"),
        P(),
    )
    relay = mesh.shape["gy"] == 2 and mesh.shape["grp"] == 4
    return jax.shard_map(
        fast_body if relay else body,
        mesh=mesh,
        in_specs=placed,
        out_specs=(
            P(None, "grp", "gx", "gy"),
            P(None, "grp", "gx", "gy"),
            P(None, "gx", ("grp", "gy")),
            P(None, None, "gx", ("grp", "gy")),
            P("gx", ("grp", "gy")),
        ),
        check_vma=False,
    )
```
